32 devices in a mesh: rep: 4 (over y, x), shard: 8 (over z, core).
Axes of the slice: x: 2, y: 2, z: 4, core: 2. Of those that a mesh axis runs over, the one named last changes fastest.
Arguments:
- inputs: bfloat16 [4, 1792, 768], P('rep', 'shard'), may hold values from -6 to 6
- cotangent: bfloat16 [4, 1792, 768], P('rep', 'shard'), may hold values from -6 to 6
- lengths: int32 [4], P('rep'), may hold values from 448 to 1792, as said below
- w_query: bfloat16 [768, 768], P('shard'), may hold values from -0.3125 to 0.3125
- w_key: bfloat16 [768, 768], P('shard'), may hold values from -0.3125 to 0.3125
- w_value: bfloat16 [768, 768], P('shard'), may hold values from -0.21875 to 0.21875
- w_out: bfloat16 [768, 768], P('shard'), may hold values from -1.25 to 1.25
- b_query: bfloat16 [768], P('shard'), may hold values from -1.5 to 1.5
- b_value: bfloat16 [768], P('shard'), may hold values from -0.25 to 0.25
- b_out: bfloat16 [768], P('shard'), may hold values from -1.5 to 1.5
- gain_one: bfloat16 [768], P('shard'), may hold values from 0.5 to 1.5
- shift_one: bfloat16 [768], P('shard'), may hold values from -1.5 to 1.5
- w_up: bfloat16 [768, 3072], P('shard'), may hold values from -0.21875 to 0.21875
- b_up: bfloat16 [3072], P('shard'), may hold values from -1.5 to 1.5
- w_down: bfloat16 [3072, 768], P('shard'), may hold values from -0.15625 to 0.15625
- b_down: bfloat16 [768], P('shard'), may hold values from -1.5 to 1.5
- gain_two: bfloat16 [768], P('shard'), may hold values from 0.5 to 1.5
- shift_two: bfloat16 [768], P('shard'), may hold values from -1.5 to 1.5
Outputs:
- layer_output: bfloat16 [4, 1792, 768], P('rep', 'shard')
- input_grad: float32 [4, 1792, 768], P('rep', 'shard')
- grad_w_query: float32 [768, 768], P('shard')
- grad_w_key: float32 [768, 768], P('shard')
- grad_w_value: float32 [768, 768], P('shard')
- grad_w_out: float32 [768, 768], P('shard')
- grad_b_query: float32 [768], P('shard')
- grad_b_value: float32 [768], P('shard')
- grad_b_out: float32 [768], P('shard')
- grad_gain_one: float32 [768], P('shard')
- grad_shift_one: float32 [768], P('shard')
- grad_w_up: float32 [768, 3072], P('shard')
- grad_b_up: float32 [3072], P('shard')
- grad_w_down: float32 [3072, 768], P('shard')
- grad_b_down: float32 [768], P('shard')
- grad_gain_two: float32 [768], P('shard')
- grad_shift_two: float32 [768], P('shard')
The draws below stay inside these ranges and needn't reach their ends.
Inputs may be any that keep to these rules, and one draw needn't show every extreme that they name: `lengths`: slot 0 is full; the others hold between a quarter of 1792 and 1792 valid tokens.
All inputs are finite; a program needn't handle non-finite values.
Results may differ from the reference program's by a relative error of at most 0.024.
Values may be sent and summed in bfloat16 or wider, within the bound.
No kernel may reach another device: no remote copies, remote signals or barrier semaphores. Data moves between devices by JAX's collectives and lax.ppermute only.
A program may use at most 256 MiB of HBM per device.

```python
import math
import jax
import jax.numpy as jnp
from jax import lax

D = 768
HEADS = 12
HEAD_DIM = 64
FF = 3072
SLOTS = 4
LEN = 1792


def draw_lengths(key, part):
    drawn = jax.random.randint(key, (SLOTS,), LEN // 4, LEN + 1, dtype=jnp.int32)
    return drawn.at[0].set(LEN)


def shard_levels(own_key, shape, cuts, least, high):
    def one(dim, parts):
        heights = jax.random.uniform(jax.random.fold_in(jax.random.fold_in(own_key, 6), dim), (parts,), jnp.float32, least / len(cuts), high / len(cuts))
        return jnp.repeat(jnp.exp(heights), shape[dim] // parts).reshape((-1,) + (1,) * (len(shape) - dim - 1))

    loudness = one(*cuts[0])
    for cut in cuts[1:]:
        loudness = loudness * one(*cut)
    return loudness


def scatter_about(stream_key, extent, deviation, reach, pieces=(), kind=jnp.bfloat16):
    loudness = shard_levels(stream_key, extent, pieces, -0.22, 0.18) if pieces else 1.0
    array = jax.random.normal(stream_key, extent, jnp.float32) * deviation * loudness
    return jnp.minimum(jnp.maximum(array, -reach), reach).astype(kind)


def setup_inputs(seed: int = 0) -> dict:
    key_list = jax.random.split(jax.random.key(seed), 19)
    inputs = scatter_about(key_list[0], (SLOTS, LEN, D), 1.0, 6.0, ((0, 4), (1, 8)))
    cotangent = scatter_about(key_list[1], (SLOTS, LEN, D), 1.0, 6.0, ((0, 4), (1, 8)))
    lengths = draw_lengths(jax.random.fold_in(key_list[18], 71), 0)
    w_query = scatter_about(key_list[3], (D, D), (D // 2) ** -0.5, 0.3125, ((0, 8),))
    w_key = scatter_about(key_list[4], (D, D), (D // 2) ** -0.5, 0.3125, ((0, 8),))
    w_value = scatter_about(key_list[5], (D, D), D ** -0.5, 0.21875, ((0, 8),))
    w_out = scatter_about(key_list[6], (D, D), (max(1, 55 * D // LEN)) ** -0.5, 1.25, ((0, 8),))
    b_query = scatter_about(key_list[7], (D,), 0.3, 1.5, ((0, 8),))
    b_value = scatter_about(key_list[8], (D,), 0.05, 0.25, ((0, 8),))
    b_out = scatter_about(key_list[9], (D,), 0.3, 1.5, ((0, 8),))
    gain_one = jnp.clip(1.0 + 0.1 * jax.random.normal(key_list[10], (D,), jnp.float32), 0.5, 1.5).astype(jnp.bfloat16)
    shift_one = scatter_about(key_list[11], (D,), 0.3, 1.5, ((0, 8),))
    w_up = scatter_about(key_list[12], (D, FF), D ** -0.5, 0.21875, ((0, 8),))
    b_up = scatter_about(key_list[13], (FF,), 0.3, 1.5, ((0, 8),))
    w_down = scatter_about(key_list[14], (FF, D), (FF // 2) ** -0.5, 0.15625, ((0, 8),))
    b_down = scatter_about(key_list[15], (D,), 0.3, 1.5, ((0, 8),))
    gain_two = jnp.clip(1.0 + 0.1 * jax.random.normal(key_list[16], (D,), jnp.float32), 0.5, 1.5).astype(jnp.bfloat16)
    shift_two = scatter_about(key_list[17], (D,), 0.3, 1.5, ((0, 8),))
    return {"inputs": inputs, "cotangent": cotangent, "lengths": lengths, "w_query": w_query, "w_key": w_key, "w_value": w_value, "w_out": w_out, "b_query": b_query, "b_value": b_value, "b_out": b_out, "gain_one": gain_one, "shift_one": shift_one, "w_up": w_up, "b_up": b_up, "w_down": w_down, "b_down": b_down, "gain_two": gain_two, "shift_two": shift_two}


@jax.custom_vjp
def low(v):
    return lax.optimization_barrier(v.astype(jnp.bfloat16)).astype(jnp.float32)

@jax.custom_vjp
def low_back(v):
    return v

def low_keep(v):
    return (low(v), None)

def low_pass(kept, grad):
    return (grad,)

def back_keep(v):
    return (v, None)

def back_low(kept, grad):
    return (low(grad),)
low.defvjp(low_keep, low_pass)
low_back.defvjp(back_keep, back_low)

def matmul(left, right):
    return jnp.dot(left, right, precision=lax.Precision.HIGHEST, preferred_element_type=jnp.float32)

def layer_norm(hidden, gain, shift):
    center = hidden - lax.optimization_barrier(jnp.mean(hidden, axis=-1, keepdims=True))
    inverse = lax.rsqrt(lax.optimization_barrier(jnp.mean(center * center, axis=-1, keepdims=True)) + 1e-05)
    return center * inverse * gain + shift

def attend(query, keys, values, valid):
    block = math.gcd(LEN, 512)
    scale = HEAD_DIM ** (-0.5)
    key_heads = keys.reshape(LEN, HEADS, HEAD_DIM)
    value_heads = values.reshape(LEN, HEADS, HEAD_DIM)
    query_blocks = query.reshape(LEN // block, block, HEADS, HEAD_DIM)

    def block_attention(query_block):
        scores = jnp.einsum('qhd,khd->hqk', query_block, key_heads, precision=lax.Precision.HIGHEST) * scale
        scores = low_back(scores)
        scores = jnp.where(valid[None, None, :], scores, -1e+30)
        probs = low(jax.nn.softmax(scores, axis=-1))
        return jnp.einsum('hqk,khd->qhd', probs, value_heads, precision=lax.Precision.HIGHEST)
    mixed = lax.map(jax.checkpoint(block_attention), query_blocks)
    return mixed.reshape(LEN, D)

def layer_out(source, params, valid):
    w_query, w_key, w_value, w_out, b_query, b_value, b_out, gain_one, shift_one, w_up, b_up, w_down, b_down, gain_two, shift_two = params
    query = low_back(low(matmul(source, w_query) + b_query))
    keys = low_back(low(matmul(source, w_key)))
    values = low_back(low(matmul(source, w_value) + b_value))
    mixed = low_back(low(attend(query, keys, values, valid)))
    branch = low_back(matmul(mixed, w_out) + b_out)
    normed = layer_norm(source + branch, gain_one, shift_one)
    upward = low_back(matmul(low(normed), w_up) + b_up)
    active = low(jax.nn.gelu(upward, approximate=False))
    second = low_back(matmul(active, w_down) + b_down)
    return layer_norm(normed + second, gain_two, shift_two)

def reference(inputs, cotangent, lengths, w_query, w_key, w_value, w_out, b_query, b_value, b_out, gain_one, shift_one, w_up, b_up, w_down, b_down, gain_two, shift_two):
    params = tuple((item.astype(jnp.float32) for item in (w_query, w_key, w_value, w_out, b_query, b_value, b_out, gain_one, shift_one, w_up, b_up, w_down, b_down, gain_two, shift_two)))

    def one_slot(totals, slot_items):
        source_bf, grad_bf, length = slot_items
        positions = jnp.arange(LEN, dtype=jnp.int32)
        valid = positions < length
        source = source_bf.astype(jnp.float32)

        def forward(source_in, params_in):
            return layer_out(source_in, params_in, valid)
        result, pullback = jax.vjp(forward, source, params)
        grad_rows = grad_bf.astype(jnp.float32) * valid[:, None].astype(jnp.float32)
        grad_source, grad_params = pullback(grad_rows)
        totals = jax.tree.map(lambda first, later: first + later, totals, grad_params)
        return (totals, (result.astype(jnp.bfloat16), grad_source))
    zeros = tuple((jnp.zeros_like(item) for item in params))
    totals, (results, grads) = lax.scan(one_slot, zeros, (inputs, cotangent, lengths))
    return (results, grads) + tuple(totals)
```

```python
import math

import jax
import jax.numpy as jnp
from jax import lax
from jax.experimental import pallas as pl
from jax.experimental.pallas import tpu as pltpu
from jax.sharding import PartitionSpec as P

HEADS = 12
HEAD_DIM = 64
SCALE = HEAD_DIM ** (-0.5)

epsilon = 1e-05
floor_value = -1e30
f32 = jnp.float32
bf16 = jnp.bfloat16


def dot(left, right, left_dim, right_dim):
    return lax.dot_general(
        left, right, (((left_dim,), (right_dim,)), ((), ())), preferred_element_type=f32
    )


def three_parts(value):
    first = value.astype(bf16)
    rest = value - first.astype(f32)
    second = rest.astype(bf16)
    third = (rest - second.astype(f32)).astype(bf16)
    return first, second, third


def extra_rows(rows, width):
    index = lax.broadcasted_iota(jnp.int32, (HEAD_DIM, width), 0)
    block = jnp.zeros((HEAD_DIM, width), f32)
    for place, row in enumerate(rows):
        block = jnp.where(index == place, row, block)
    return block.astype(bf16)


def forward_kernel(q_ref, kv_ref, aug_ref, o_ref, ot_ref, lse_ref, acc_ref, max_ref, sum_ref, *, block):
    width = q_ref.shape[0]
    heads = width // HEAD_DIM
    keys = kv_ref.shape[1]
    queries = q_ref.shape[1]
    unit = extra_rows([1.0], queries)
    wide = [
        jnp.concatenate([q_ref[h * HEAD_DIM : (h + 1) * HEAD_DIM, :], unit], axis=0)
        for h in range(heads)
    ]
    acc_ref[...] = jnp.zeros(acc_ref.shape, f32)
    sum_ref[...] = jnp.zeros(sum_ref.shape, f32)
    max_ref[...] = jnp.full(max_ref.shape, 2 * floor_value, f32)

    def step(index, carry):
        span = pl.ds(pl.multiple_of(index * block, block), block)
        aug = aug_ref[:, span]
        for h in range(heads):
            part = slice(h * HEAD_DIM, (h + 1) * HEAD_DIM)
            key = jnp.concatenate([kv_ref[part, span], aug], axis=0).T
            scores = dot(key, wide[h], 1, 0)
            old = max_ref[h : h + 1, :]
            newest = jnp.maximum(old, jnp.max(scores, axis=0, keepdims=True))
            alpha = jnp.exp(old - newest)
            weights = jnp.exp(scores - newest)
            max_ref[h : h + 1, :] = newest
            sum_ref[h : h + 1, :] = sum_ref[h : h + 1, :] * alpha + jnp.sum(
                weights, axis=0, keepdims=True
            )
            value = kv_ref[width + h * HEAD_DIM : width + (h + 1) * HEAD_DIM, span]
            acc_ref[part, :] = acc_ref[part, :] * alpha + dot(value, weights.astype(bf16), 1, 0)
        return carry

    lax.fori_loop(0, keys // block, step, 0)
    for h in range(heads):
        part = slice(h * HEAD_DIM, (h + 1) * HEAD_DIM)
        total = sum_ref[h : h + 1, :]
        ot_ref[part, :] = acc_ref[part, :] / total
        lse_ref[h : h + 1, :] = max_ref[h : h + 1, :] + jnp.log(total)
    o_ref[...] = ot_ref[...].astype(bf16).T


def backward_kernel(q_ref, kv_ref, aug_ref, ot_ref, lse_ref, do_ref, dq_ref, dk_ref, dv_ref, acc_ref, *, block):
    width = q_ref.shape[0]
    heads = width // HEAD_DIM
    keys = kv_ref.shape[1]
    queries = q_ref.shape[1]
    out_grad = do_ref[...]
    out_grad_t = out_grad.T
    query = q_ref[...].T
    lane = lax.broadcasted_iota(jnp.int32, query.shape, 1) // HEAD_DIM
    only_q = [jnp.where(lane == h, query, jnp.zeros_like(query)) for h in range(heads)]
    only_do = [jnp.where(lane == h, out_grad, jnp.zeros_like(query)) for h in range(heads)]
    wide_q = []
    wide_do = []
    for h in range(heads):
        part = slice(h * HEAD_DIM, (h + 1) * HEAD_DIM)
        lse = [-piece.astype(f32) for piece in three_parts(lse_ref[h : h + 1, :])]
        wide_q.append(jnp.concatenate([q_ref[part, :], extra_rows([1.0] + lse, queries)], axis=0))
        delta = jnp.sum(out_grad_t[part, :].astype(f32) * ot_ref[part, :], axis=0, keepdims=True)
        pieces = [-piece.astype(f32) for piece in three_parts(delta)]
        wide_do.append(
            jnp.concatenate([out_grad_t[part, :], extra_rows([0.0] + pieces, queries)], axis=0)
        )
    acc_ref[...] = jnp.zeros(acc_ref.shape, f32)

    def step(index, carry):
        span = pl.ds(pl.multiple_of(index * block, block), block)
        aug = aug_ref[:, span]
        grad_key = jnp.zeros((block, width), f32)
        grad_value = jnp.zeros((block, width), f32)
        for h in range(heads):
            part = slice(h * HEAD_DIM, (h + 1) * HEAD_DIM)
            key_t = kv_ref[part, span]
            value_t = kv_ref[width + h * HEAD_DIM : width + (h + 1) * HEAD_DIM, span]
            key = jnp.concatenate([key_t, aug], axis=0).T
            value = jnp.concatenate([value_t, aug], axis=0).T
            probs = jnp.exp(dot(key, wide_q[h], 1, 0))
            centred = dot(value, wide_do[h], 1, 0)
            low = probs.astype(bf16)
            scores = (probs * centred).astype(bf16)
            grad_key += dot(scores, only_q[h], 1, 0)
            grad_value += dot(low, only_do[h], 1, 0)
            acc_ref[part, :] += dot(key_t, scores, 1, 0)
        dk_ref[span, :] = grad_key.astype(bf16)
        dv_ref[span, :] = grad_value.astype(bf16)
        return carry

    lax.fori_loop(0, keys // block, step, 0)
    dq_ref[...] = (acc_ref[...] * SCALE).astype(bf16).T


def attend_forward(query, pairs, aug):
    width, queries = query.shape
    keys = pairs.shape[1]
    block = math.gcd(keys, 256)
    return pl.pallas_call(
        lambda *refs: forward_kernel(*refs, block=block),
        out_shape=(
            jax.ShapeDtypeStruct((queries, width), bf16),
            jax.ShapeDtypeStruct((width, queries), f32),
            jax.ShapeDtypeStruct((8, queries), f32),
        ),
        scratch_shapes=[
            pltpu.VMEM((width, queries), f32),
            pltpu.VMEM((8, queries), f32),
            pltpu.VMEM((8, queries), f32),
        ],
        name="attend_forward",
    )(query, pairs, aug)


def attend_backward(query, pairs, aug, mixed_t, lse, out_grad):
    width, queries = query.shape
    keys = pairs.shape[1]
    block = math.gcd(keys, 256)
    return pl.pallas_call(
        lambda *refs: backward_kernel(*refs, block=block),
        out_shape=(
            jax.ShapeDtypeStruct((queries, width), bf16),
            jax.ShapeDtypeStruct((keys, width), bf16),
            jax.ShapeDtypeStruct((keys, width), bf16),
        ),
        scratch_shapes=[pltpu.VMEM((width, queries), f32)],
        name="attend_backward",
    )(query, pairs, aug, mixed_t, lse, out_grad)


def norm_forward(hidden, gain, shift):
    center = hidden - jnp.mean(hidden, axis=1, keepdims=True)
    inverse = lax.rsqrt(jnp.mean(center * center, axis=1, keepdims=True) + epsilon)
    scaled = center * inverse
    return (scaled * gain.astype(f32) + shift.astype(f32), scaled, inverse)


def norm_backward(grad_out, gain, scaled, inverse):
    grad_scaled = grad_out * gain.astype(f32)
    grad_in = inverse * (
        grad_scaled
        - jnp.mean(grad_scaled, axis=1, keepdims=True)
        - scaled * jnp.mean(grad_scaled * scaled, axis=1, keepdims=True)
    )
    return (grad_in, jnp.sum(grad_out * scaled, axis=0), jnp.sum(grad_out, axis=0))


def gelu_both(upward):
    cumulative = 0.5 * (1.0 + lax.erf(upward * 0.7071067811865476))
    density = jnp.exp(-0.5 * upward * upward) * 0.3989422804014327
    return (upward * cumulative, cumulative + upward * density)


def column_sum(values_low):
    return jnp.sum(values_low.astype(f32), axis=0)


def make_body(reps, shards):
    groups = math.gcd(HEADS, shards)
    peers = shards // groups

    def swap_group(value, e):
        perm = [(s, s ^ (e * peers)) for s in range(shards)]
        return lax.ppermute(value, "shard", perm)

    def swap_peer(value, d):
        perm = [(s, s ^ d) for s in range(shards)]
        return lax.ppermute(value, "shard", perm)

    def across_reps(value):
        return lax.all_to_all(value, "rep", 0, 0, tiled=True)

    def body(
        inputs,
        cotangent,
        lengths,
        w_query,
        w_key,
        w_value,
        w_out,
        b_query,
        b_value,
        b_out,
        gain_one,
        shift_one,
        w_up,
        b_up,
        w_down,
        b_down,
        gain_two,
        shift_two,
    ):
        tokens = inputs[0]
        rows, model = tokens.shape
        width = model // groups
        small_rows = w_query.shape[0]
        hidden_rows = w_down.shape[0]
        length = lengths[0]
        shard = lax.axis_index("shard")
        group = shard // peers
        peer = shard % peers
        own_valid = shard * rows + jnp.arange(rows, dtype=jnp.int32) < length
        row_valid = own_valid.astype(f32)
        source = tokens.astype(f32)

        blocks = [tokens]
        for e in range(1, groups):
            blocks.append(swap_group(tokens, e))
        x = jnp.concatenate(blocks, axis=0)

        packed = jnp.stack([w_query, w_key, w_value])
        packed = packed.reshape(3, small_rows, groups, width).transpose(2, 0, 1, 3)
        zg = [[g * peers + p for g in range(groups)] for p in range(peers)]
        got = lax.all_to_all(packed, "shard", 0, 0, tiled=True, axis_index_groups=zg)
        got = [got] + [swap_peer(got, d) for d in range(1, peers)]
        order = peer ^ jnp.arange(peers)
        bias = jnp.stack([b_query, b_value])
        bias = jnp.stack([bias] + [swap_peer(bias, d) for d in range(1, peers)])[order]
        bias = bias.transpose(1, 0, 2).reshape(2, width)
        w_heads = jnp.stack(got)[order].transpose(2, 1, 0, 3, 4).reshape(3, model, width)

        w_all = lax.all_gather(
            jnp.concatenate(
                [
                    w_out,
                    jnp.concatenate(
                        [
                            b_out,
                            gain_one,
                            shift_one,
                            b_up,
                            b_down,
                            gain_two,
                            shift_two,
                            jnp.zeros((-(6 * small_rows + b_up.shape[0])) % model, bf16),
                        ]
                    ).reshape(-1, model),
                ]
            ),
            "shard",
            axis=0,
        )
        out_full = w_all[:, :small_rows].reshape(model, model)
        flat = w_all[:, small_rows:].reshape(shards, -1)
        bounds = []
        start = 0
        for item in (b_out, gain_one, shift_one, b_up, b_down, gain_two, shift_two):
            bounds.append(flat[:, start : start + item.shape[0]].reshape(-1))
            start += item.shape[0]
        bias_out, gain_first, shift_first, bias_up, bias_down, gain_second, shift_second = bounds
        up_full = lax.all_gather(w_up, "shard", axis=0, tiled=True)
        down_full = lax.all_gather(w_down, "shard", axis=0, tiled=True)

        query_t = ((dot(w_heads[0], x, 0, 1) + bias[0].astype(f32)[:, None]).astype(bf16)) * SCALE
        key_t = dot(w_heads[1], x, 0, 1).astype(bf16)
        value_t = (dot(w_heads[2], x, 0, 1) + bias[1].astype(f32)[:, None]).astype(bf16)
        pair = jnp.concatenate([key_t, value_t], axis=0)
        pairs = jnp.concatenate([pair] + [swap_peer(pair, d) for d in range(1, peers)], axis=1)
        starts = (
            (group ^ jnp.arange(groups))[None, :] * peers + (peer ^ jnp.arange(peers))[:, None]
        ) * rows
        positions = (starts[:, :, None] + jnp.arange(rows)[None, None, :]).reshape(1, -1)
        keys = positions.shape[1]
        aug = jnp.concatenate(
            [
                jnp.where(positions < length, 0.0, floor_value).astype(bf16),
                jnp.ones((3, keys), bf16),
                jnp.zeros((HEAD_DIM - 4, keys), bf16),
            ]
        )
        heads_low, mixed_t, lse = attend_forward(query_t, pairs, aug)

        def to_tokens(value):
            pieces = value.reshape((groups, rows) + value.shape[1:])
            got = [pieces[0]] + [swap_group(pieces[e], e) for e in range(1, groups)]
            return jnp.stack(got)[group ^ jnp.arange(groups)]

        def to_heads(value):
            value = value[group ^ jnp.arange(groups)]
            got = [value[0]] + [swap_group(value[e], e) for e in range(1, groups)]
            return jnp.concatenate(got, axis=0)

        mixed_low = to_tokens(heads_low).transpose(1, 0, 2).reshape(rows, model)
        branch = dot(mixed_low, out_full, 1, 0) + bias_out.astype(f32)
        normed, scaled_one, inverse_one = norm_forward(source + branch, gain_first, shift_first)
        normed_low = normed.astype(bf16)
        upward = dot(normed_low, up_full, 1, 0) + bias_up.astype(f32)
        active, slope = gelu_both(upward)
        active_low = active.astype(bf16)
        second = dot(active_low, down_full, 1, 0) + bias_down.astype(f32)
        result, scaled_two, inverse_two = norm_forward(normed + second, gain_second, shift_second)

        grad_result = cotangent[0].astype(f32) * row_valid[:, None]
        grad_sum_two, grad_gain_second, grad_shift_second = norm_backward(
            grad_result, gain_second, scaled_two, inverse_two
        )
        grad_second = grad_sum_two.astype(bf16)
        grad_down = dot(active_low, grad_second, 0, 0)
        grad_bias_down = column_sum(grad_second)
        grad_upward = (dot(grad_second, down_full, 1, 1) * slope).astype(bf16)
        grad_up = dot(normed_low, grad_upward, 0, 0)
        grad_bias_up = column_sum(grad_upward)
        grad_normed = grad_sum_two + dot(grad_upward, up_full, 1, 1)
        grad_sum_one, grad_gain_first, grad_shift_first = norm_backward(
            grad_normed, gain_first, scaled_one, inverse_one
        )
        grad_branch = grad_sum_one.astype(bf16)
        grad_out_proj = dot(mixed_low, grad_branch, 0, 0)
        grad_bias_out = column_sum(grad_branch)
        grad_mixed = dot(grad_branch, out_full, 1, 1).astype(bf16)
        grad_heads = to_heads(grad_mixed.reshape(rows, groups, width).transpose(1, 0, 2))

        dq, dk, dv = attend_backward(query_t, pairs, aug, mixed_t, lse, grad_heads)
        dkv = jnp.concatenate([dk, dv], axis=1)
        class_rows = groups * rows
        total = dkv[:class_rows].astype(f32)
        for d in range(1, peers):
            total += swap_peer(dkv[d * class_rows : (d + 1) * class_rows], d).astype(f32)
        dqkv = jnp.concatenate([dq, total.astype(bf16)], axis=1)

        w_joined = w_heads.transpose(1, 0, 2).reshape(model, 3 * width)
        partial = dot(dqkv, w_joined, 1, 1).astype(bf16).reshape(groups, rows, model)
        grad_input = grad_sum_one + partial[0].astype(f32)
        for e in range(1, groups):
            grad_input += swap_group(partial[e], e).astype(f32)

        grad_heads_w = dot(x, dqkv, 0, 0).astype(bf16).reshape(shards, small_rows, 3 * width)
        spread = lax.all_to_all(grad_heads_w, "shard", 0, 0, tiled=True)
        spread = spread.reshape(groups, peers, small_rows, 3, width).astype(f32).sum(axis=1)
        part_heads = spread.transpose(2, 1, 0, 3).reshape(3 * small_rows, model)

        scatter = lambda value: lax.psum_scatter(
            value.astype(bf16), "shard", scatter_dimension=0, tiled=True
        ).astype(f32)
        part_out = scatter(grad_out_proj)
        part_up = scatter(grad_up).reshape(small_rows, -1, model)
        part_down = scatter(grad_down)
        parts = jnp.concatenate(
            [
                part_heads,
                part_out,
                part_up.transpose(1, 0, 2).reshape(-1, model),
                part_down,
            ]
        ).astype(bf16)
        shared = across_reps(parts).reshape((reps, -1, model)).astype(f32).sum(axis=0)
        shared = across_reps(
            jnp.broadcast_to(shared.astype(bf16)[None], (reps,) + shared.shape).reshape(-1, model)
        ).astype(f32)
        sum_query, sum_key, sum_value, sum_out = (
            shared[i * small_rows : (i + 1) * small_rows] for i in range(4)
        )
        up_rows = small_rows * (w_up.shape[1] // model)
        sum_up = shared[4 * small_rows : 4 * small_rows + up_rows]
        sum_up = sum_up.reshape(-1, small_rows, model).transpose(1, 0, 2).reshape(w_up.shape)
        sum_down = shared[4 * small_rows + up_rows :]

        head_bias = jnp.stack([column_sum(dqkv[:, :width]), column_sum(dqkv[:, 2 * width :])])
        placed = jnp.zeros((2, groups, width), f32)
        placed = lax.dynamic_update_slice(placed, head_bias[:, None], (0, group, 0))
        vectors = [placed[0].reshape(-1), placed[1].reshape(-1)] + [
            grad_bias_out,
            grad_gain_first,
            grad_shift_first,
            grad_bias_up,
            grad_bias_down,
            grad_gain_second,
            grad_shift_second,
        ]
        sizes = [v.shape[0] // shards for v in vectors]
        stacked = jnp.concatenate([v.reshape(shards, -1) for v in vectors], axis=1)
        every = jnp.broadcast_to(stacked[None], (reps,) + stacked.shape).reshape(-1, stacked.shape[1])
        every = lax.all_to_all(every, ("rep", "shard"), 0, 0, tiled=True).sum(axis=0)
        sums = []
        start = 0
        for size in sizes:
            sums.append(every[start : start + size])
            start += size
        return (
            result.astype(bf16)[None],
            grad_input[None],
            sum_query,
            sum_key,
            sum_value,
            sum_out,
            sums[0],
            sums[1],
            sums[2],
            sums[3],
            sums[4],
            sum_up,
            sums[5],
            sum_down,
            sums[6],
            sums[7],
            sums[8],
        )

    return body


def solution(mesh):
    rows, vector, token = P("shard", None), P("shard"), P("rep", "shard", None)
    params = (rows,) * 4 + (vector,) * 5 + (rows, vector, rows) + (vector,) * 3
    return jax.shard_map(
        make_body(mesh.shape["rep"], mesh.shape["shard"]),
        mesh=mesh,
        in_specs=(token, token, P("rep")) + params,
        out_specs=(token, token) + params,
        check_vma=False,
    )
```
